512 devices in a mesh: grp: 8 (over z_hi, x), tm: 64 (over y, z_lo, core).
Axes of the slice: x: 4, y: 4, z: 16 (z_hi: 2, z_lo: 8; z = z_hi * 8 + z_lo), core: 2. Of those that a mesh axis runs over, the one named last changes fastest.
Arguments:
- residual: bfloat16 [8, 8192, 1536], P('grp', 'tm'), may hold values from -6 to 6
- queries: bfloat16 [8, 8192, 1536], P('grp', 'tm'), may hold values from -16 to 16
- key_rows: bfloat16 [8, 8192, 1536], P('grp', 'tm'), may hold values from -6 to 6
- value_rows: bfloat16 [8, 8192, 1536], P('grp', 'tm'), may hold values from -6 to 6
- conv_weight: float32 [31, 1536], replicated, may hold values from -1 to 1
- lengths: int32 [8], P('grp'), may hold values from 4096 to 8192
- frame_lang: int32 [8, 8192], P('grp', 'tm'), may hold values from 0 to 7, as said below
- up_weight: bfloat16 [8, 1536, 6144], P('grp', None, 'tm'), may hold values from -0.15625 to 0.15625
- down_weight: bfloat16 [8, 6144, 1536], P('grp', 'tm'), may hold values from -0.078125 to 0.078125
Outputs:
- output: bfloat16 [8, 8192, 1536], P('grp', 'tm')
The draws below stay inside these ranges and needn't reach their ends.
Inputs may be any that keep to these rules, and one draw needn't show every extreme that they name: `frame_lang`: the language of the segment that holds each frame.
All inputs are finite; a program needn't handle non-finite values.
Results may differ from the reference program's by a relative error of at most 0.0095.
Values may be sent and summed in bfloat16 or wider, within the bound.
A program may use at most 64 MiB of HBM per device.

```python
import math
import jax
import jax.numpy as jnp
from jax import lax

D = 1536
HEAD = 128
FF = 6144
KERNEL = 31
WIN = 128
F_DEV = 128
SEQS = 8
EXPERTS = 8
FRAMES = 8192
CAP = 20
N_TM = 64


def frame_language(key):
    folded = jax.random.fold_in(key, 11)
    span_key, first_key, second_key, order_key = jax.random.split(folded, 4)
    seg_count = FRAMES // 4 + 1
    seg_spans = jax.random.randint(span_key, (SEQS, seg_count), 4, 25, dtype=jnp.int32)
    seg_ends = jnp.cumsum(seg_spans, axis=1)
    frame_pos = jnp.arange(FRAMES, dtype=jnp.int32)
    segment = jax.vmap(lambda row_ends: jnp.searchsorted(row_ends, frame_pos, side='right'))(seg_ends).astype(jnp.int32)
    first_rank = jax.random.randint(first_key, (SEQS, seg_count), 0, EXPERTS, dtype=jnp.int32)
    second_rank = jax.random.randint(second_key, (SEQS, seg_count), 0, EXPERTS, dtype=jnp.int32)
    lang_rank = jnp.minimum(first_rank, second_rank)
    lang_order = jax.random.permutation(order_key, EXPERTS).astype(jnp.int32)
    seg_lang = lang_order[lang_rank]
    return jnp.take_along_axis(seg_lang, segment, axis=1).astype(jnp.int32)


def attention_pair(key):
    folded = jax.random.fold_in(key, 23)
    key_draw, query_draw = jax.random.split(folded)
    array_shape = (SEQS, FRAMES, D)
    key_out = jnp.clip(jax.random.normal(key_draw, array_shape, jnp.float32), -6.0, 6.0)
    query_out = jnp.clip(jax.random.normal(query_draw, array_shape, jnp.float32), -6.0, 6.0)
    return (query_out, key_out)


def draw_queries(key, part):
    return attention_pair(key)[0].astype(jnp.bfloat16)


def draw_key_rows(key, part):
    return attention_pair(key)[1].astype(jnp.bfloat16)


def draw_frame_lang(key, part):
    return frame_language(key)


def with_ends(values, key, low, top_value):
    longest = values.shape.index(max(values.shape))
    spots = []
    for shift in (0, 1):
        where = [jax.random.randint(jax.random.fold_in(key, axis), (), 0, length) for axis, length in enumerate(values.shape)]
        where[longest] = (where[longest] + shift) % values.shape[longest]
        spots.append(tuple(where))
    return values.at[spots[0]].set(low).at[spots[1]].set(top_value)


def block_scale(key, dims, cuts, low, largest):
    def one(position, shards_of):
        draws = jax.random.uniform(jax.random.fold_in(jax.random.fold_in(key, 6), position), (shards_of,), jnp.float32, low / len(cuts), largest / len(cuts))
        return jnp.repeat(jnp.exp(draws), dims[position] // shards_of).reshape((-1,) + (1,) * (len(dims) - position - 1))

    level = one(*cuts[0])
    for cut in cuts[1:]:
        level = level * one(*cut)
    return level


def scatter_about(key, extent, width, most, cuts=(), kind=jnp.bfloat16):
    values = width * jax.random.normal(key, extent, jnp.float32)
    if cuts:
        values = values * block_scale(key, extent, cuts, -0.22, 0.18)
    return jnp.clip(values, -most, most).astype(kind)


def setup_inputs(seed: int = 0) -> dict:
    streams_of = jax.random.split(jax.random.key(seed), 10)
    residual = scatter_about(streams_of[0], (SEQS, FRAMES, D), 1.0, 6.0, ((0, 8), (1, 64)))
    queries = draw_queries(jax.random.fold_in(streams_of[9], 71), 0)
    key_rows = draw_key_rows(jax.random.fold_in(streams_of[9], 71), 0)
    value_rows = scatter_about(streams_of[3], (SEQS, FRAMES, D), 1.0, 6.0, ((0, 8), (1, 64)))
    conv_weight = scatter_about(streams_of[4], (KERNEL, D), KERNEL ** -0.5, 1.0, (), jnp.float32)
    lengths = with_ends(jax.random.randint(streams_of[5], (SEQS,), FRAMES // 2, FRAMES + 1), jax.random.fold_in(streams_of[5], 1), FRAMES // 2, FRAMES).astype(jnp.int32)
    frame_lang = draw_frame_lang(jax.random.fold_in(streams_of[9], 71), 0)
    up_weight = scatter_about(streams_of[7], (EXPERTS, D, FF), D ** -0.5, 0.15625, ((0, 8), (2, 64)))
    down_weight = scatter_about(streams_of[8], (EXPERTS, FF, D), FF ** -0.5, 0.078125, ((0, 8), (1, 64)))
    return {"residual": residual, "queries": queries, "key_rows": key_rows, "value_rows": value_rows, "conv_weight": conv_weight, "lengths": lengths, "frame_lang": frame_lang, "up_weight": up_weight, "down_weight": down_weight}


def layer_norm(values):
    row_mean = lax.optimization_barrier(jnp.mean(values, axis=-1, keepdims=True))
    centred = values - row_mean
    spread = lax.optimization_barrier(jnp.mean(centred * centred, axis=-1, keepdims=True))
    return centred * lax.rsqrt(spread + 1e-05)

def attend_block(query_block, key_block, value_block, query_pos, key_pos, length):
    head_count = D // HEAD
    query_heads = query_block.astype(jnp.float32).reshape(-1, head_count, HEAD)
    key_heads = key_block.astype(jnp.float32).reshape(-1, head_count, HEAD)
    value_heads = value_block.astype(jnp.float32).reshape(-1, head_count, HEAD)
    scores = jnp.einsum('ihd,jhd->hij', query_heads, key_heads) / math.sqrt(HEAD)
    in_window = jnp.abs(query_pos[:, None] - key_pos[None, :]) <= WIN
    is_live = ((key_pos >= 0) & (key_pos < length))[None, :] | (query_pos[:, None] == key_pos[None, :])
    allowed = (in_window & is_live)[None, :, :]
    row_top = lax.optimization_barrier(jnp.max(jnp.where(allowed, scores, -jnp.inf), axis=-1, keepdims=True))
    weights = jnp.where(allowed, jnp.exp(scores - row_top), 0.0)
    attn_probs = (weights / lax.optimization_barrier(jnp.sum(weights, axis=-1, keepdims=True))).astype(jnp.bfloat16)
    head_mix = jnp.einsum('hij,jhd->ihd', attn_probs.astype(jnp.float32), value_heads)
    return head_mix.reshape(query_block.shape[0], D).astype(jnp.bfloat16)

def group_section(residual, queries, key_rows, value_rows, length, conv_weight):
    frame_pos = jnp.arange(FRAMES, dtype=jnp.int32)
    is_valid = frame_pos < length
    margin = ((WIN, WIN), (0, 0))
    key_pad = jnp.pad(key_rows, margin)
    value_pad = jnp.pad(value_rows, margin)

    def one_block(block_index):
        block_start = (block_index * F_DEV).astype(jnp.int32)
        query_block = lax.dynamic_slice_in_dim(queries, block_start, F_DEV, 0)
        key_block = lax.dynamic_slice_in_dim(key_pad, block_start, F_DEV + 2 * WIN, 0)
        value_block = lax.dynamic_slice_in_dim(value_pad, block_start, F_DEV + 2 * WIN, 0)
        query_pos = block_start + jnp.arange(F_DEV, dtype=jnp.int32)
        key_pos = block_start - WIN + jnp.arange(F_DEV + 2 * WIN, dtype=jnp.int32)
        return attend_block(query_block, key_block, value_block, query_pos, key_pos, length)
    attended = lax.map(one_block, jnp.arange(FRAMES // F_DEV, dtype=jnp.int32)).reshape(FRAMES, D)
    middle = (residual.astype(jnp.float32) + attended.astype(jnp.float32)).astype(jnp.bfloat16)
    normed = (layer_norm(middle.astype(jnp.float32)) * is_valid[:, None]).astype(jnp.bfloat16)
    conv_reach = (KERNEL - 1) // 2
    padded = jnp.pad(normed.astype(jnp.float32), ((conv_reach, conv_reach), (0, 0)))
    conv_sum = jnp.zeros((FRAMES, D), jnp.float32)
    for kernel_tap in range(KERNEL):
        conv_sum = conv_sum + conv_weight[kernel_tap] * padded[kernel_tap:kernel_tap + FRAMES]
    conv_out = (middle.astype(jnp.float32) + jax.nn.silu(conv_sum)).astype(jnp.bfloat16)
    ffn_in = layer_norm(conv_out.astype(jnp.float32)).astype(jnp.bfloat16)
    return (conv_out, ffn_in, is_valid)

def reference(residual, queries, key_rows, value_rows, conv_weight, lengths, frame_lang, up_weight, down_weight):

    def section(items):
        return group_section(items[0], items[1], items[2], items[3], items[4], conv_weight)
    conv_out, ffn_in, is_valid = lax.map(section, (residual, queries, key_rows, value_rows, lengths))
    onehot = ((frame_lang[..., None] == jnp.arange(EXPERTS, dtype=jnp.int32)) & is_valid[..., None]).astype(jnp.int32)
    blocks = onehot.reshape(SEQS, N_TM, F_DEV, EXPERTS)
    before = jnp.cumsum(blocks, axis=2) - blocks
    slot_index = lax.optimization_barrier(jnp.sum(before * blocks, axis=-1)).reshape(SEQS, FRAMES)
    is_kept = is_valid & (slot_index < CAP)
    block_of = jnp.arange(FRAMES, dtype=jnp.int32) // F_DEV
    seq_ids = jnp.arange(SEQS, dtype=jnp.int32)
    target = ((seq_ids[:, None] * N_TM + block_of[None, :]) * CAP + slot_index).reshape(-1)
    buffer_rows = SEQS * N_TM * CAP
    flat_in = jnp.concatenate([ffn_in.reshape(-1, D), jnp.zeros((1, D), jnp.bfloat16)], axis=0)
    flat_lang = frame_lang.reshape(-1)
    flat_kept = is_kept.reshape(-1)
    frame_ids = jnp.arange(SEQS * FRAMES, dtype=jnp.int32)

    def one_expert(carry, items):
        up_block, down_block, expert_id = items
        chosen = flat_kept & (flat_lang == expert_id)
        dest = jnp.where(chosen, target, buffer_rows).astype(jnp.int32)
        source = jnp.full((buffer_rows + 1,), SEQS * FRAMES, jnp.int32).at[dest].set(frame_ids)
        gathered = flat_in[source[:buffer_rows]]
        hidden = jax.nn.silu(jnp.dot(gathered, up_block, preferred_element_type=jnp.float32)).astype(jnp.bfloat16)
        result = jnp.dot(hidden, down_block, preferred_element_type=jnp.float32).astype(jnp.bfloat16)
        result = jnp.concatenate([result, jnp.zeros((1, D), jnp.bfloat16)], axis=0)
        carry = jnp.where(chosen[:, None], result[dest], carry)
        return (carry, None)
    expert_out, unused = lax.scan(one_expert, jnp.zeros((SEQS * FRAMES, D), jnp.bfloat16), (up_weight, down_weight, jnp.arange(EXPERTS, dtype=jnp.int32)))
    expert_out = expert_out.reshape(SEQS, FRAMES, D)
    output = is_valid[..., None] * (conv_out.astype(jnp.float32) + 0.5 * expert_out.astype(jnp.float32))
    return output.astype(jnp.bfloat16)
```

```python
import math

import jax
import jax.numpy as jnp
from jax import lax
from jax.sharding import PartitionSpec as P

HEAD = 128
WIN = 128


def with_halo(cells, sides, width):
    for axis, dim in sides:
        count = lax.axis_size(axis)
        ends = count - 1
        head = lax.slice_in_dim(cells, 0, width, axis=dim)
        tail = lax.slice_in_dim(cells, cells.shape[dim] - width, cells.shape[dim], axis=dim)
        cells = jnp.concatenate(
            [
                lax.ppermute(tail, axis, [(i, (i + 1) % count) for i in range(ends)]),
                cells,
                lax.ppermute(head, axis, [((i + 1) % count, i) for i in range(ends)]),
            ],
            axis=dim,
        )
    return cells


def layer_norm(values):
    row_mean = jnp.mean(values, axis=-1, keepdims=True)
    centred = values - row_mean
    spread = jnp.mean(centred * centred, axis=-1, keepdims=True)
    return centred * lax.rsqrt(spread + 1e-05)


def time_rim(source, rim_width):
    return with_halo(source, (("tm", 0),), rim_width)


def ring_step(array, stride, count, places, shift):
    return lax.ppermute(
        array, "tm", [(i, i + stride * ((i // stride + shift) % count - i // stride)) for i in range(places)]
    )


def gather_rows(own, stride, count, places):
    half = own.shape[0] // 2
    before = ring_step(own, stride, count, places, 1)
    after = ring_step(own, stride, count, places, -1)
    far_top = ring_step(before[:half], stride, count, places, 1)
    far_low = ring_step(after[half:], stride, count, places, -1)
    return before, after, jnp.concatenate([far_top, far_low], axis=0)


def fold_rows(own, before, after, far, stride, count, places):
    half = own.shape[0] // 2
    narrow = lambda v: v.astype(jnp.bfloat16)
    wide = lambda v: v.astype(jnp.float32)
    from_before = ring_step(narrow(far[:half]), stride, count, places, 1)
    from_after = ring_step(narrow(far[half:]), stride, count, places, -1)
    after = jnp.concatenate([after[:half] + wide(from_before), after[half:]], axis=0)
    before = jnp.concatenate([before[:half], before[half:] + wide(from_after)], axis=0)
    one = ring_step(narrow(after), stride, count, places, 1)
    two = ring_step(narrow(before), stride, count, places, -1)
    return own + wide(one) + wide(two)


def expert(rows, up_rows, down_rows):
    hidden = lax.dot_general(
        rows, up_rows, (((1,), (1,)), ((), ())), preferred_element_type=jnp.float32
    )
    hidden = jax.nn.silu(hidden).astype(jnp.bfloat16)
    return jnp.dot(hidden, down_rows, preferred_element_type=jnp.float32)


def attend(query_rows, widened, query_pos, key_pos, length):
    frames, model_width = query_rows.shape
    head_count = model_width // HEAD
    query_heads = query_rows.reshape(frames, head_count, HEAD)
    key_heads = widened[:, 0].reshape(-1, head_count, HEAD)
    value_heads = widened[:, 1].reshape(-1, head_count, HEAD)
    scores = jnp.einsum(
        "ihd,jhd->hij", query_heads, key_heads, preferred_element_type=jnp.float32
    ) / math.sqrt(HEAD)
    in_window = jnp.abs(query_pos[:, None] - key_pos[None, :]) <= WIN
    is_live = ((key_pos >= 0) & (key_pos < length))[None, :] | (
        query_pos[:, None] == key_pos[None, :]
    )
    allowed = (in_window & is_live)[None, :, :]
    row_top = jnp.max(jnp.where(allowed, scores, -jnp.inf), axis=-1, keepdims=True)
    weights = jnp.where(allowed, jnp.exp(scores - row_top), 0.0)
    attn_probs = (weights / jnp.sum(weights, axis=-1, keepdims=True)).astype(jnp.bfloat16)
    head_mix = jnp.einsum(
        "hij,jhd->ihd", attn_probs, value_heads, preferred_element_type=jnp.float32
    )
    return head_mix.reshape(frames, model_width).astype(jnp.bfloat16)


def body(
    residual,
    queries,
    key_rows,
    value_rows,
    conv_weight,
    lengths,
    frame_lang,
    up_weight,
    down_weight,
):
    frames = residual.shape[1]
    model_width = residual.shape[2]
    conv_reach = (conv_weight.shape[0] - 1) // 2
    tm_place = lax.axis_index("tm")
    places = lax.axis_size("tm")
    ring = 4
    stride = places // ring
    experts = lax.axis_size("grp")
    slot_count = 5 * frames // (4 * experts)
    units = down_weight.shape[1]
    shard = jnp.concatenate([up_weight[0].T, down_weight[0]], axis=0)
    weights = lax.all_gather(
        shard,
        "tm",
        axis_index_groups=[[g * stride + i for i in range(stride)] for g in range(ring)],
    )
    frame_start = tm_place * frames
    query_pos = frame_start + jnp.arange(frames, dtype=jnp.int32)
    key_pos = frame_start - WIN + jnp.arange(frames + 2 * WIN, dtype=jnp.int32)
    length = lengths[0]
    is_valid = query_pos < length
    key_value = jnp.stack([key_rows[0], value_rows[0]], axis=1)
    widened = time_rim(key_value, WIN)
    attended = attend(queries[0], widened, query_pos, key_pos, length)
    middle = (residual[0].astype(jnp.float32) + attended.astype(jnp.float32)).astype(jnp.bfloat16)
    normed = (layer_norm(middle.astype(jnp.float32)) * is_valid[:, None]).astype(jnp.bfloat16)
    beside_all = time_rim(normed, conv_reach)
    conv_sum = jnp.zeros((frames, model_width), jnp.float32)
    for kernel_tap in range(conv_weight.shape[0]):
        conv_sum = conv_sum + conv_weight[kernel_tap] * beside_all[
            kernel_tap : kernel_tap + frames
        ].astype(jnp.float32)
    conv_out = (middle.astype(jnp.float32) + jax.nn.silu(conv_sum)).astype(jnp.bfloat16)
    ffn_in = layer_norm(conv_out.astype(jnp.float32)).astype(jnp.bfloat16)
    language = frame_lang[0]
    onehot = (
        (language[:, None] == jnp.arange(experts, dtype=jnp.int32)[None, :]) & is_valid[:, None]
    ).astype(jnp.int32)
    earlier = jnp.cumsum(onehot, axis=0) - onehot
    slot_index = jnp.sum(earlier * onehot, axis=1)
    is_kept = is_valid & (slot_index < slot_count)
    target = language * slot_count + slot_index
    route_table = (
        (target[None, :] == jnp.arange(experts * slot_count, dtype=jnp.int32)[:, None])
        & is_kept[None, :]
    ).astype(jnp.bfloat16)
    outgoing = jnp.dot(route_table, ffn_in, preferred_element_type=jnp.float32).astype(jnp.bfloat16)
    outgoing = outgoing.reshape(experts, slot_count, model_width)
    arrived = lax.all_to_all(outgoing, "grp", split_axis=0, concat_axis=0, tiled=True)
    item_count = arrived.shape[1]
    frame_rows = arrived.reshape(-1, model_width)
    before, after, far = gather_rows(frame_rows, stride, ring, places)
    up_rows = weights[:, :units].reshape(-1, model_width)
    down_rows = weights[:, units:].reshape(-1, model_width)
    all_rows = jnp.concatenate([frame_rows, before, after, far], axis=0)
    partial_value = expert(all_rows, up_rows, down_rows).reshape(4, -1, model_width)
    total = fold_rows(*partial_value, stride, ring, places)
    outbound = total.astype(jnp.bfloat16).reshape(experts, item_count, model_width)
    returned = lax.all_to_all(outbound, "grp", split_axis=0, concat_axis=0, tiled=True)
    expert_out = lax.dot_general(
        route_table,
        returned.reshape(-1, model_width),
        (((0,), (0,)), ((), ())),
        preferred_element_type=jnp.float32,
    )
    output = is_valid[:, None] * (conv_out.astype(jnp.float32) + 0.5 * expert_out)
    return output.astype(jnp.bfloat16)[None]


def solution(mesh):
    in_specs = (
        P("grp", "tm", None),
        P("grp", "tm", None),
        P("grp", "tm", None),
        P("grp", "tm", None),
        P(),
        P("grp"),
        P("grp", "tm"),
        P("grp", None, "tm"),
        P("grp", "tm", None),
    )
    out_specs = P("grp", "tm", None)
    return jax.shard_map(body, mesh=mesh, in_specs=in_specs, out_specs=out_specs, check_vma=False)
```

```python
import math

import jax
import jax.numpy as jnp
from jax import lax
from jax.sharding import PartitionSpec as P

HEAD = 128
WIN = 128


def with_halo(cells, sides, width):
    for axis, dim in sides:
        count = lax.axis_size(axis)
        ends = count - 1
        head = lax.slice_in_dim(cells, 0, width, axis=dim)
        tail = lax.slice_in_dim(cells, cells.shape[dim] - width, cells.shape[dim], axis=dim)
        cells = jnp.concatenate(
            [
                lax.ppermute(tail, axis, [(i, (i + 1) % count) for i in range(ends)]),
                cells,
                lax.ppermute(head, axis, [((i + 1) % count, i) for i in range(ends)]),
            ],
            axis=dim,
        )
    return cells


def layer_norm(values):
    row_mean = jnp.mean(values, axis=-1, keepdims=True)
    centred = values - row_mean
    spread = jnp.mean(centred * centred, axis=-1, keepdims=True)
    return centred * lax.rsqrt(spread + 1e-05)


def time_rim(source, rim_width):
    return with_halo(source, (("tm", 0),), rim_width)


def ring_step(array, stride, count, places, shift):
    return lax.ppermute(
        array, "tm", [(i, i + stride * ((i // stride + shift) % count - i // stride)) for i in range(places)]
    )


def gather_rows(own, stride, count, places):
    half = own.shape[0] // 2
    before = ring_step(own, stride, count, places, 1)
    after = ring_step(own, stride, count, places, -1)
    far_top = ring_step(before[:half], stride, count, places, 1)
    far_low = ring_step(after[half:], stride, count, places, -1)
    return own, before, after, jnp.concatenate([far_top, far_low], axis=0)


def fold_rows(own, before, after, far, stride, count, places):
    half = own.shape[1] // 2
    narrow = lambda v: v.astype(jnp.bfloat16)
    wide = lambda v: v.astype(jnp.float32)
    from_before = ring_step(narrow(far[:, :half]), stride, count, places, 1)
    from_after = ring_step(narrow(far[:, half:]), stride, count, places, -1)
    after = jnp.concatenate([after[:, :half] + wide(from_before), after[:, half:]], axis=1)
    before = jnp.concatenate([before[:, :half], before[:, half:] + wide(from_after)], axis=1)
    one = ring_step(narrow(after), stride, count, places, 1)
    two = ring_step(narrow(before), stride, count, places, -1)
    return narrow(own + wide(one) + wide(two))


def group_hop(array, hop, groups, places, stride, is_return):
    count = groups // 2
    pairs = []
    for group in range(groups):
        for place in range(places):
            is_other, ahead = hop // count, hop % count
            there = (group // count ^ is_other) * count + (group % count + ahead) % count
            row, spot = place // stride, place % stride
            if is_other:
                spot = (stride // 2 - 1 - spot // 2) * 2 + spot % 2
            pair = (group * places + place, there * places + row * stride + spot)
            pairs.append(pair[::-1] if is_return else pair)
    return lax.ppermute(array, ("grp", "tm"), pairs)


def attend(query_rows, widened, query_pos, key_pos, length):
    frames, model_width = query_rows.shape
    head_count = model_width // HEAD
    query_heads = query_rows.reshape(frames, head_count, HEAD)
    key_heads = widened[:, 0].reshape(-1, head_count, HEAD)
    value_heads = widened[:, 1].reshape(-1, head_count, HEAD)
    scores = jnp.einsum(
        "ihd,jhd->hij", query_heads, key_heads, preferred_element_type=jnp.float32
    ) / math.sqrt(HEAD)
    in_window = jnp.abs(query_pos[:, None] - key_pos[None, :]) <= WIN
    is_live = ((key_pos >= 0) & (key_pos < length))[None, :] | (
        query_pos[:, None] == key_pos[None, :]
    )
    allowed = (in_window & is_live)[None, :, :]
    row_top = jnp.max(jnp.where(allowed, scores, -jnp.inf), axis=-1, keepdims=True)
    weights = jnp.where(allowed, jnp.exp(scores - row_top), 0.0)
    attn_probs = (weights / jnp.sum(weights, axis=-1, keepdims=True)).astype(jnp.bfloat16)
    head_mix = jnp.einsum(
        "hij,jhd->ihd", attn_probs, value_heads, preferred_element_type=jnp.float32
    )
    return head_mix.reshape(frames, model_width).astype(jnp.bfloat16)


def body(
    residual,
    queries,
    key_rows,
    value_rows,
    conv_weight,
    lengths,
    frame_lang,
    up_weight,
    down_weight,
):
    frames = residual.shape[1]
    model_width = residual.shape[2]
    conv_reach = (conv_weight.shape[0] - 1) // 2
    tm_place = lax.axis_index("tm")
    places = lax.axis_size("tm")
    ring = 4
    stride = places // ring
    experts = lax.axis_size("grp")
    slot_count = 5 * frames // (4 * experts)
    lines = [[g * stride + i for i in range(stride)] for g in range(ring)]
    up_rows = lax.all_gather(up_weight[0].T, "tm", axis_index_groups=lines, tiled=True)
    down_rows = lax.all_gather(down_weight[0], "tm", axis_index_groups=lines, tiled=True)
    frame_start = tm_place * frames
    query_pos = frame_start + jnp.arange(frames, dtype=jnp.int32)
    key_pos = frame_start - WIN + jnp.arange(frames + 2 * WIN, dtype=jnp.int32)
    length = lengths[0]
    is_valid = query_pos < length
    key_value = jnp.stack([key_rows[0], value_rows[0]], axis=1)
    widened = time_rim(key_value, WIN)
    attended = attend(queries[0], widened, query_pos, key_pos, length)
    middle = (residual[0].astype(jnp.float32) + attended.astype(jnp.float32)).astype(jnp.bfloat16)
    normed = (layer_norm(middle.astype(jnp.float32)) * is_valid[:, None]).astype(jnp.bfloat16)
    beside_all = time_rim(normed, conv_reach)
    conv_sum = jnp.zeros((frames, model_width), jnp.float32)
    for kernel_tap in range(conv_weight.shape[0]):
        conv_sum = conv_sum + conv_weight[kernel_tap] * beside_all[
            kernel_tap : kernel_tap + frames
        ].astype(jnp.float32)
    conv_out = (middle.astype(jnp.float32) + jax.nn.silu(conv_sum)).astype(jnp.bfloat16)
    ffn_in = layer_norm(conv_out.astype(jnp.float32)).astype(jnp.bfloat16)
    language = frame_lang[0]
    onehot = (
        (language[:, None] == jnp.arange(experts, dtype=jnp.int32)[None, :]) & is_valid[:, None]
    ).astype(jnp.int32)
    earlier = jnp.cumsum(onehot, axis=0) - onehot
    slot_index = jnp.sum(earlier * onehot, axis=1)
    is_kept = is_valid & (slot_index < slot_count)
    group = lax.axis_index("grp")
    count = experts // 2
    relative = (language // count ^ group // count) * count + (language - group) % count
    target = relative * slot_count + slot_index
    route_table = (
        (target[None, :] == jnp.arange(experts * slot_count, dtype=jnp.int32)[:, None])
        & is_kept[None, :]
    ).astype(jnp.bfloat16)
    outgoing = jnp.dot(route_table, ffn_in, preferred_element_type=jnp.float32).astype(jnp.bfloat16)
    outgoing = outgoing.reshape(experts, slot_count, model_width)
    hops = [*range(count, experts), *range(1, count)]
    arrived = {0: outgoing[0]}
    for hop in hops:
        arrived[hop] = group_hop(outgoing[hop], hop, experts, places, stride, False)
    frame_rows = jnp.concatenate([arrived[hop] for hop in range(experts)], axis=0)
    blocks = gather_rows(frame_rows, stride, ring, places)
    half = frame_rows.shape[0] // 2
    all_rows = jnp.concatenate([rows[half:] for rows in blocks] + [rows[:half] for rows in blocks], axis=0)
    hidden = lax.dot_general(all_rows, up_rows, (((1,), (1,)), ((), ())), preferred_element_type=jnp.float32)
    hidden = jax.nn.silu(hidden).astype(jnp.bfloat16)

    def finish(hidden_rows):
        partial = jnp.dot(hidden_rows, down_rows, preferred_element_type=jnp.float32)
        total = fold_rows(*partial.reshape(ring, half, model_width), stride, ring, places)
        return total.reshape(count, slot_count, model_width)

    far_total = finish(hidden[: ring * half])
    returned = {}
    for hop in range(count, experts):
        returned[hop] = group_hop(far_total[hop - count], hop, experts, places, stride, True)
    near_total = finish(hidden[ring * half :])
    returned[0] = near_total[0]
    for hop in range(1, count):
        returned[hop] = group_hop(near_total[hop], hop, experts, places, stride, True)
    returned = jnp.concatenate([returned[hop] for hop in range(experts)], axis=0)
    expert_out = lax.dot_general(
        route_table,
        returned,
        (((0,), (0,)), ((), ())),
        preferred_element_type=jnp.float32,
    )
    output = is_valid[:, None] * (conv_out.astype(jnp.float32) + 0.5 * expert_out)
    return output.astype(jnp.bfloat16)[None]


def solution(mesh):
    in_specs = (
        P("grp", "tm", None),
        P("grp", "tm", None),
        P("grp", "tm", None),
        P("grp", "tm", None),
        P(),
        P("grp"),
        P("grp", "tm"),
        P("grp", None, "tm"),
        P("grp", "tm", None),
    )
    out_specs = P("grp", "tm", None)
    return jax.shard_map(body, mesh=mesh, in_specs=in_specs, out_specs=out_specs, check_vma=False)
```

```python
import math

import jax
import jax.numpy as jnp
from jax import lax
from jax.experimental import pallas as pl
from jax.experimental.pallas import tpu as pltpu
from jax.sharding import PartitionSpec as P

HEAD = 128
WIN = 128


def with_halo(cells, sides, width):
    for axis, dim in sides:
        count = lax.axis_size(axis)
        ends = count - 1
        head = lax.slice_in_dim(cells, 0, width, axis=dim)
        tail = lax.slice_in_dim(cells, cells.shape[dim] - width, cells.shape[dim], axis=dim)
        cells = jnp.concatenate(
            [
                lax.ppermute(tail, axis, [(i, (i + 1) % count) for i in range(ends)]),
                cells,
                lax.ppermute(head, axis, [((i + 1) % count, i) for i in range(ends)]),
            ],
            axis=dim,
        )
    return cells


def layer_norm(values):
    row_mean = jnp.mean(values, axis=-1, keepdims=True)
    centred = values - row_mean
    spread = jnp.mean(centred * centred, axis=-1, keepdims=True)
    return centred * lax.rsqrt(spread + 1e-05)


def time_rim(source, rim_width):
    return with_halo(source, (("tm", 0),), rim_width)


def place_hop(array, places, to):
    return lax.ppermute(array, "tm", [(i, to(i)) for i in range(places)])


def group_hop(array, ahead, is_other, groups, places, stride, is_return):
    count = groups // 2
    pairs = []
    for group in range(groups):
        for place in range(places):
            there = (group // count ^ is_other) * count + (group % count + ahead) % count
            row, spot = place // stride, place % stride
            if is_other:
                spot = (stride // 2 - 1 - spot // 2) * 2 + spot % 2
            pair = (group * places + place, there * places + row * stride + spot)
            pairs.append(pair[::-1] if is_return else pair)
    return lax.ppermute(array, ("grp", "tm"), pairs)


def expert_kernel(rows_ref, weights_ref, out_ref):
    shards, twice, width = weights_ref.shape
    units = twice // 2
    up = weights_ref[:, :units, :].reshape(shards * units, width)
    down = weights_ref[:, units:, :].reshape(shards * units, width)
    hidden = lax.dot_general(
        rows_ref[...], up, (((1,), (1,)), ((), ())), preferred_element_type=jnp.float32
    )
    hidden = (hidden / (1.0 + jnp.exp(-hidden))).astype(jnp.bfloat16)
    part = jnp.dot(hidden, down, preferred_element_type=jnp.float32)

    @pl.when(pl.program_id(0) == 0)
    def _():
        out_ref[...] = part

    @pl.when(pl.program_id(0) > 0)
    def _():
        out_ref[...] += part


def expert(rows, weights, step=4):
    count, width = rows.shape
    shards, twice, _ = weights.shape
    return pl.pallas_call(
        expert_kernel,
        grid=(shards // step,),
        in_specs=[
            pl.BlockSpec((count, width), lambda i: (0, 0)),
            pl.BlockSpec((step, twice, width), lambda i: (i, 0, 0)),
        ],
        out_specs=pl.BlockSpec((count, width), lambda i: (0, 0)),
        out_shape=jax.ShapeDtypeStruct((count, width), jnp.float32),
        cost_estimate=pl.CostEstimate(
            flops=2 * count * width * shards * twice,
            bytes_accessed=2 * weights.size + 6 * rows.size,
            transcendentals=count * shards * twice // 2,
        ),
        compiler_params=pltpu.CompilerParams(vmem_limit_bytes=40 * 2**20),
    )(rows, weights)


def attend(query_rows, widened, query_pos, key_pos, length):
    frames, model_width = query_rows.shape
    head_count = model_width // HEAD
    query_heads = query_rows.reshape(frames, head_count, HEAD)
    key_heads = widened[:, 0].reshape(-1, head_count, HEAD)
    value_heads = widened[:, 1].reshape(-1, head_count, HEAD)
    scores = jnp.einsum(
        "ihd,jhd->hij", query_heads, key_heads, preferred_element_type=jnp.float32
    ) / math.sqrt(HEAD)
    in_window = jnp.abs(query_pos[:, None] - key_pos[None, :]) <= WIN
    is_live = ((key_pos >= 0) & (key_pos < length))[None, :] | (
        query_pos[:, None] == key_pos[None, :]
    )
    allowed = (in_window & is_live)[None, :, :]
    row_top = jnp.max(jnp.where(allowed, scores, -jnp.inf), axis=-1, keepdims=True)
    weights = jnp.where(allowed, jnp.exp(scores - row_top), 0.0)
    attn_probs = (weights / jnp.sum(weights, axis=-1, keepdims=True)).astype(jnp.bfloat16)
    head_mix = jnp.einsum(
        "hij,jhd->ihd", attn_probs, value_heads, preferred_element_type=jnp.float32
    )
    return head_mix.reshape(frames, model_width).astype(jnp.bfloat16)


def body(
    residual,
    queries,
    key_rows,
    value_rows,
    conv_weight,
    lengths,
    frame_lang,
    up_weight,
    down_weight,
):
    frames = residual.shape[1]
    model_width = residual.shape[2]
    conv_reach = (conv_weight.shape[0] - 1) // 2
    tm_place = lax.axis_index("tm")
    places = lax.axis_size("tm")
    ring = 4
    stride = places // ring
    experts = lax.axis_size("grp")
    slot_count = 5 * frames // (4 * experts)
    shard = jnp.concatenate([up_weight[0].T, down_weight[0]], axis=0)
    loops = []
    for pair in range(ring // 2):
        for core in range(2):
            up_line = [2 * pair * stride + z * 2 + core for z in range(stride // 2)]
            loops.append(up_line + [i + stride for i in up_line[::-1]])
    weights = lax.all_gather(shard, "tm", axis_index_groups=loops)
    frame_start = tm_place * frames
    query_pos = frame_start + jnp.arange(frames, dtype=jnp.int32)
    key_pos = frame_start - WIN + jnp.arange(frames + 2 * WIN, dtype=jnp.int32)
    length = lengths[0]
    is_valid = query_pos < length
    key_value = jnp.stack([key_rows[0], value_rows[0]], axis=1)
    widened = time_rim(key_value, WIN)
    attended = attend(queries[0], widened, query_pos, key_pos, length)
    middle = (residual[0].astype(jnp.float32) + attended.astype(jnp.float32)).astype(jnp.bfloat16)
    normed = (layer_norm(middle.astype(jnp.float32)) * is_valid[:, None]).astype(jnp.bfloat16)
    beside_all = time_rim(normed, conv_reach)
    conv_sum = jnp.zeros((frames, model_width), jnp.float32)
    for kernel_tap in range(conv_weight.shape[0]):
        conv_sum = conv_sum + conv_weight[kernel_tap] * beside_all[
            kernel_tap : kernel_tap + frames
        ].astype(jnp.float32)
    conv_out = (middle.astype(jnp.float32) + jax.nn.silu(conv_sum)).astype(jnp.bfloat16)
    ffn_in = layer_norm(conv_out.astype(jnp.float32)).astype(jnp.bfloat16)
    language = frame_lang[0]
    onehot = (
        (language[:, None] == jnp.arange(experts, dtype=jnp.int32)[None, :]) & is_valid[:, None]
    ).astype(jnp.int32)
    earlier = jnp.cumsum(onehot, axis=0) - onehot
    slot_index = jnp.sum(earlier * onehot, axis=1)
    is_kept = is_valid & (slot_index < slot_count)
    group = lax.axis_index("grp")
    count = experts // 2
    relative = (language - group) % count * 2 + (language // count ^ group // count)
    target = relative * slot_count + slot_index
    route_table = (
        (target[None, :] == jnp.arange(experts * slot_count, dtype=jnp.int32)[:, None])
        & is_kept[None, :]
    ).astype(jnp.bfloat16)
    outgoing = jnp.dot(route_table, ffn_in, preferred_element_type=jnp.float32).astype(jnp.bfloat16)
    hop = lambda v, ahead, is_other, is_return: group_hop(
        v, ahead, is_other, experts, places, stride, is_return
    )
    outgoing = outgoing.reshape(count, 2, slot_count, model_width)
    near = jnp.stack([outgoing[0]] + [hop(outgoing[i], i, 0, False) for i in range(1, count)])
    half = count * slot_count
    far_rows = hop(near[:, 1].reshape(half, model_width), 0, 1, False)
    own = jnp.concatenate([far_rows, near[:, 0].reshape(half, model_width)], axis=0)
    across = lambda i: (ring - 1 - i // stride) * stride + i % stride
    beside = lambda i: i ^ 1
    pair_rows = jnp.stack([own, place_hop(own, places, across)])
    all_rows = jnp.stack([pair_rows, place_hop(pair_rows, places, beside)])
    all_rows = all_rows.reshape(4, 2, half, model_width).swapaxes(0, 1).reshape(-1, model_width)
    partial = expert(all_rows, weights).reshape(2, 2, 2, half, model_width)

    def fold(part):
        mine = part[0] + place_hop(part[1].astype(jnp.bfloat16), places, beside).astype(jnp.float32)
        other = place_hop(mine[1].astype(jnp.bfloat16), places, across).astype(jnp.float32)
        return (mine[0] + other).astype(jnp.bfloat16)

    far_back = hop(fold(partial[0]), 0, 1, True).reshape(count, slot_count, model_width)
    near_back = fold(partial[1]).reshape(count, slot_count, model_width)
    back = jnp.stack([near_back, far_back], axis=1)
    returned = jnp.stack([back[0]] + [hop(back[i], i, 0, True) for i in range(1, count)])
    expert_out = lax.dot_general(
        route_table,
        returned.reshape(-1, model_width),
        (((0,), (0,)), ((), ())),
        preferred_element_type=jnp.float32,
    )
    output = is_valid[:, None] * (conv_out.astype(jnp.float32) + 0.5 * expert_out)
    return output.astype(jnp.bfloat16)[None]


def solution(mesh):
    in_specs = (
        P("grp", "tm", None),
        P("grp", "tm", None),
        P("grp", "tm", None),
        P("grp", "tm", None),
        P(),
        P("grp"),
        P("grp", "tm"),
        P("grp", None, "tm"),
        P("grp", "tm", None),
    )
    out_specs = P("grp", "tm", None)
    return jax.shard_map(body, mesh=mesh, in_specs=in_specs, out_specs=out_specs, check_vma=False)
```

```python
import math

import jax
import jax.numpy as jnp
from jax import lax
from jax.experimental import pallas as pl
from jax.experimental.pallas import tpu as pltpu
from jax.sharding import PartitionSpec as P

HEAD = 128
WIN = 128


def with_halo(cells, sides, width):
    for axis, dim in sides:
        count = lax.axis_size(axis)
        ends = count - 1
        head = lax.slice_in_dim(cells, 0, width, axis=dim)
        tail = lax.slice_in_dim(cells, cells.shape[dim] - width, cells.shape[dim], axis=dim)
        cells = jnp.concatenate(
            [
                lax.ppermute(tail, axis, [(i, (i + 1) % count) for i in range(ends)]),
                cells,
                lax.ppermute(head, axis, [((i + 1) % count, i) for i in range(ends)]),
            ],
            axis=dim,
        )
    return cells


def layer_norm(values):
    row_mean = jnp.mean(values, axis=-1, keepdims=True)
    centred = values - row_mean
    spread = jnp.mean(centred * centred, axis=-1, keepdims=True)
    return centred * lax.rsqrt(spread + 1e-05)


def time_rim(source, rim_width):
    return with_halo(source, (("tm", 0),), rim_width)


def place_hop(array, places, to):
    return lax.ppermute(array, "tm", [(i, to(i)) for i in range(places)])


def group_hop(array, ahead, is_other, groups, places, stride, is_return):
    count = groups // 2
    pairs = []
    for group in range(groups):
        for place in range(places):
            there = (group // count ^ is_other) * count + (group % count + ahead) % count
            row, spot = place // stride, place % stride
            if is_other:
                spot = (stride // 2 - 1 - spot // 2) * 2 + spot % 2
            pair = (group * places + place, there * places + row * stride + spot)
            pairs.append(pair[::-1] if is_return else pair)
    return lax.ppermute(array, ("grp", "tm"), pairs)


def expert_kernel(rows_ref, weights_ref, out_ref):
    shards, twice, width = weights_ref.shape
    units = twice // 2
    up = weights_ref[:, :units, :].reshape(shards * units, width)
    down = weights_ref[:, units:, :].reshape(shards * units, width)
    hidden = lax.dot_general(
        rows_ref[...], up, (((1,), (1,)), ((), ())), preferred_element_type=jnp.float32
    )
    hidden = (hidden / (1.0 + jnp.exp(-hidden))).astype(jnp.bfloat16)
    part = jnp.dot(hidden, down, preferred_element_type=jnp.float32)

    @pl.when(pl.program_id(0) == 0)
    def _():
        out_ref[...] = part

    @pl.when(pl.program_id(0) > 0)
    def _():
        out_ref[...] += part


def expert(rows, weights, step=8):
    count, width = rows.shape
    shards, twice, _ = weights.shape
    return pl.pallas_call(
        expert_kernel,
        grid=(shards // step,),
        in_specs=[
            pl.BlockSpec((count, width), lambda i: (0, 0)),
            pl.BlockSpec((step, twice, width), lambda i: (i, 0, 0)),
        ],
        out_specs=pl.BlockSpec((count, width), lambda i: (0, 0)),
        out_shape=jax.ShapeDtypeStruct((count, width), jnp.float32),
        cost_estimate=pl.CostEstimate(
            flops=2 * count * width * shards * twice,
            bytes_accessed=2 * weights.size + 6 * rows.size,
            transcendentals=count * shards * twice // 2,
        ),
        compiler_params=pltpu.CompilerParams(vmem_limit_bytes=51 * 2**20),
    )(rows, weights)


def attend(query_rows, widened, query_pos, key_pos, length):
    frames, model_width = query_rows.shape
    head_count = model_width // HEAD
    query_heads = query_rows.reshape(frames, head_count, HEAD)
    key_heads = widened[:, 0].reshape(-1, head_count, HEAD)
    value_heads = widened[:, 1].reshape(-1, head_count, HEAD)
    scores = jnp.einsum(
        "ihd,jhd->hij", query_heads, key_heads, preferred_element_type=jnp.float32
    ) / math.sqrt(HEAD)
    in_window = jnp.abs(query_pos[:, None] - key_pos[None, :]) <= WIN
    is_live = ((key_pos >= 0) & (key_pos < length))[None, :] | (
        query_pos[:, None] == key_pos[None, :]
    )
    allowed = (in_window & is_live)[None, :, :]
    row_top = jnp.max(jnp.where(allowed, scores, -jnp.inf), axis=-1, keepdims=True)
    weights = jnp.where(allowed, jnp.exp(scores - row_top), 0.0)
    attn_probs = (weights / jnp.sum(weights, axis=-1, keepdims=True)).astype(jnp.bfloat16)
    head_mix = jnp.einsum(
        "hij,jhd->ihd", attn_probs, value_heads, preferred_element_type=jnp.float32
    )
    return head_mix.reshape(frames, model_width).astype(jnp.bfloat16)


def body(
    residual,
    queries,
    key_rows,
    value_rows,
    conv_weight,
    lengths,
    frame_lang,
    up_weight,
    down_weight,
):
    frames = residual.shape[1]
    model_width = residual.shape[2]
    conv_reach = (conv_weight.shape[0] - 1) // 2
    tm_place = lax.axis_index("tm")
    places = lax.axis_size("tm")
    ring = 4
    stride = places // ring
    experts = lax.axis_size("grp")
    slot_count = 5 * frames // (4 * experts)
    shard = jnp.concatenate([up_weight[0].T, down_weight[0]], axis=0)
    loops = []
    for pair in range(ring // 2):
        for core in range(2):
            up_line = [2 * pair * stride + z * 2 + core for z in range(stride // 2)]
            loops.append(up_line + [i + stride for i in up_line[::-1]])
    weights = lax.all_gather(shard, "tm", axis_index_groups=loops)
    frame_start = tm_place * frames
    query_pos = frame_start + jnp.arange(frames, dtype=jnp.int32)
    key_pos = frame_start - WIN + jnp.arange(frames + 2 * WIN, dtype=jnp.int32)
    length = lengths[0]
    is_valid = query_pos < length
    key_value = jnp.stack([key_rows[0], value_rows[0]], axis=1)
    widened = time_rim(key_value, WIN)
    attended = attend(queries[0], widened, query_pos, key_pos, length)
    middle = (residual[0].astype(jnp.float32) + attended.astype(jnp.float32)).astype(jnp.bfloat16)
    normed = (layer_norm(middle.astype(jnp.float32)) * is_valid[:, None]).astype(jnp.bfloat16)
    beside_all = time_rim(normed, conv_reach)
    conv_sum = jnp.zeros((frames, model_width), jnp.float32)
    for kernel_tap in range(conv_weight.shape[0]):
        conv_sum = conv_sum + conv_weight[kernel_tap] * beside_all[
            kernel_tap : kernel_tap + frames
        ].astype(jnp.float32)
    conv_out = (middle.astype(jnp.float32) + jax.nn.silu(conv_sum)).astype(jnp.bfloat16)
    ffn_in = layer_norm(conv_out.astype(jnp.float32)).astype(jnp.bfloat16)
    language = frame_lang[0]
    onehot = (
        (language[:, None] == jnp.arange(experts, dtype=jnp.int32)[None, :]) & is_valid[:, None]
    ).astype(jnp.int32)
    earlier = jnp.cumsum(onehot, axis=0) - onehot
    slot_index = jnp.sum(earlier * onehot, axis=1)
    is_kept = is_valid & (slot_index < slot_count)
    group = lax.axis_index("grp")
    count = experts // 2
    relative = (language - group) % count * 2 + (language // count ^ group // count)
    target = relative * slot_count + slot_index
    route_table = (
        (target[None, :] == jnp.arange(experts * slot_count, dtype=jnp.int32)[:, None])
        & is_kept[None, :]
    ).astype(jnp.bfloat16)
    outgoing = jnp.dot(route_table, ffn_in, preferred_element_type=jnp.float32).astype(jnp.bfloat16)
    hop = lambda v, ahead, is_other, is_return: group_hop(
        v, ahead, is_other, experts, places, stride, is_return
    )
    outgoing = outgoing.reshape(count, 2, slot_count, model_width)
    near = jnp.stack([outgoing[0]] + [hop(outgoing[i], i, 0, False) for i in range(1, count)])
    half = count * slot_count
    far_rows = hop(near[:, 1].reshape(half, model_width), 0, 1, False)
    own = jnp.concatenate([far_rows, near[:, 0].reshape(half, model_width)], axis=0)
    across = lambda i: (ring - 1 - i // stride) * stride + i % stride
    beside = lambda i: i ^ 1
    pair_rows = jnp.stack([own, place_hop(own, places, across)])
    all_rows = jnp.stack([pair_rows, place_hop(pair_rows, places, beside)])
    all_rows = all_rows.reshape(4, 2, half, model_width)

    def finish(part):
        partial = expert(all_rows[:, part].reshape(-1, model_width), weights)
        partial = partial.reshape(2, 2, half, model_width)
        mine = partial[0] + place_hop(partial[1].astype(jnp.bfloat16), places, beside).astype(jnp.float32)
        other = place_hop(mine[1].astype(jnp.bfloat16), places, across).astype(jnp.float32)
        return (mine[0] + other).astype(jnp.bfloat16).reshape(count, slot_count, model_width)

    far_total = finish(0)
    far_back = [hop(far_total[i], i, 1, True) for i in range(count)]
    near_total = finish(1)
    near_back = [near_total[0]] + [hop(near_total[i], i, 0, True) for i in range(1, count)]
    returned = jnp.stack([jnp.stack(pair) for pair in zip(near_back, far_back)])
    expert_out = lax.dot_general(
        route_table,
        returned.reshape(-1, model_width),
        (((0,), (0,)), ((), ())),
        preferred_element_type=jnp.float32,
    )
    output = is_valid[:, None] * (conv_out.astype(jnp.float32) + 0.5 * expert_out)
    return output.astype(jnp.bfloat16)[None]


def solution(mesh):
    in_specs = (
        P("grp", "tm", None),
        P("grp", "tm", None),
        P("grp", "tm", None),
        P("grp", "tm", None),
        P(),
        P("grp"),
        P("grp", "tm"),
        P("grp", None, "tm"),
        P("grp", "tm", None),
    )
    out_specs = P("grp", "tm", None)
    return jax.shard_map(body, mesh=mesh, in_specs=in_specs, out_specs=out_specs, check_vma=False)
```

```python
import math

import jax
import jax.numpy as jnp
from jax import lax
from jax.experimental import pallas as pl
from jax.experimental.pallas import tpu as pltpu
from jax.sharding import PartitionSpec as P

HEAD = 128
WIN = 128


def with_halo(cells, sides, width):
    for axis, dim in sides:
        count = lax.axis_size(axis)
        ends = count - 1
        head = lax.slice_in_dim(cells, 0, width, axis=dim)
        tail = lax.slice_in_dim(cells, cells.shape[dim] - width, cells.shape[dim], axis=dim)
        cells = jnp.concatenate(
            [
                lax.ppermute(tail, axis, [(i, (i + 1) % count) for i in range(ends)]),
                cells,
                lax.ppermute(head, axis, [((i + 1) % count, i) for i in range(ends)]),
            ],
            axis=dim,
        )
    return cells


def layer_norm(values):
    row_mean = jnp.mean(values, axis=-1, keepdims=True)
    centred = values - row_mean
    spread = jnp.mean(centred * centred, axis=-1, keepdims=True)
    return centred * lax.rsqrt(spread + 1e-05)


def time_rim(source, rim_width):
    return with_halo(source, (("tm", 0),), rim_width)


def place_hop(array, places, to):
    return lax.ppermute(array, "tm", [(i, to(i)) for i in range(places)])


def group_hop(array, ahead, is_other, groups, places, stride, is_return):
    count = groups // 2
    pairs = []
    for group in range(groups):
        for place in range(places):
            there = (group // count ^ is_other) * count + (group % count + ahead) % count
            row, spot = place // stride, place % stride
            if is_other:
                spot = (stride // 2 - 1 - spot // 2) * 2 + spot % 2
            pair = (group * places + place, there * places + row * stride + spot)
            pairs.append(pair[::-1] if is_return else pair)
    return lax.ppermute(array, ("grp", "tm"), pairs)


def expert_kernel(rows_ref, weights_ref, out_ref):
    shards, twice, width = weights_ref.shape
    units = twice // 2
    up = weights_ref[:, :units, :].reshape(shards * units, width)
    down = weights_ref[:, units:, :].reshape(shards * units, width)
    hidden = lax.dot_general(
        rows_ref[...], up, (((1,), (1,)), ((), ())), preferred_element_type=jnp.float32
    )
    hidden = (hidden / (1.0 + jnp.exp(-hidden))).astype(jnp.bfloat16)
    part = jnp.dot(hidden, down, preferred_element_type=jnp.float32)

    @pl.when(pl.program_id(0) == 0)
    def _():
        out_ref[...] = part

    @pl.when(pl.program_id(0) > 0)
    def _():
        out_ref[...] += part


def expert(rows, weights, step=8):
    count, width = rows.shape
    shards, twice, _ = weights.shape
    return pl.pallas_call(
        expert_kernel,
        grid=(shards // step,),
        in_specs=[
            pl.BlockSpec((count, width), lambda i: (0, 0)),
            pl.BlockSpec((step, twice, width), lambda i: (i, 0, 0)),
        ],
        out_specs=pl.BlockSpec((count, width), lambda i: (0, 0)),
        out_shape=jax.ShapeDtypeStruct((count, width), jnp.float32),
        cost_estimate=pl.CostEstimate(
            flops=2 * count * width * shards * twice,
            bytes_accessed=2 * weights.size + 6 * rows.size,
            transcendentals=count * shards * twice // 2,
        ),
        compiler_params=pltpu.CompilerParams(vmem_limit_bytes=40 * 2**20),
    )(rows, weights)


def attend(query_rows, widened, query_pos, key_pos, length):
    frames, model_width = query_rows.shape
    head_count = model_width // HEAD
    query_heads = query_rows.reshape(frames, head_count, HEAD)
    key_heads = widened[:, 0].reshape(-1, head_count, HEAD)
    value_heads = widened[:, 1].reshape(-1, head_count, HEAD)
    scores = jnp.einsum(
        "ihd,jhd->hij", query_heads, key_heads, preferred_element_type=jnp.float32
    ) / math.sqrt(HEAD)
    in_window = jnp.abs(query_pos[:, None] - key_pos[None, :]) <= WIN
    is_live = ((key_pos >= 0) & (key_pos < length))[None, :] | (
        query_pos[:, None] == key_pos[None, :]
    )
    allowed = (in_window & is_live)[None, :, :]
    row_top = jnp.max(jnp.where(allowed, scores, -jnp.inf), axis=-1, keepdims=True)
    weights = jnp.where(allowed, jnp.exp(scores - row_top), 0.0)
    attn_probs = (weights / jnp.sum(weights, axis=-1, keepdims=True)).astype(jnp.bfloat16)
    head_mix = jnp.einsum(
        "hij,jhd->ihd", attn_probs, value_heads, preferred_element_type=jnp.float32
    )
    return head_mix.reshape(frames, model_width).astype(jnp.bfloat16)


def body(
    residual,
    queries,
    key_rows,
    value_rows,
    conv_weight,
    lengths,
    frame_lang,
    up_weight,
    down_weight,
):
    frames = residual.shape[1]
    model_width = residual.shape[2]
    conv_reach = (conv_weight.shape[0] - 1) // 2
    tm_place = lax.axis_index("tm")
    places = lax.axis_size("tm")
    ring = 4
    stride = places // ring
    experts = lax.axis_size("grp")
    slot_count = 5 * frames // (4 * experts)
    shard = jnp.concatenate([up_weight[0].T, down_weight[0]], axis=0)
    loops = []
    for pair in range(ring // 2):
        for core in range(2):
            up_line = [2 * pair * stride + z * 2 + core for z in range(stride // 2)]
            loops.append(up_line + [i + stride for i in up_line[::-1]])
    weights = lax.all_gather(shard, "tm", axis_index_groups=loops)
    frame_start = tm_place * frames
    query_pos = frame_start + jnp.arange(frames, dtype=jnp.int32)
    key_pos = frame_start - WIN + jnp.arange(frames + 2 * WIN, dtype=jnp.int32)
    length = lengths[0]
    is_valid = query_pos < length
    key_value = jnp.stack([key_rows[0], value_rows[0]], axis=1)
    widened = time_rim(key_value, WIN)
    attended = attend(queries[0], widened, query_pos, key_pos, length)
    middle = (residual[0].astype(jnp.float32) + attended.astype(jnp.float32)).astype(jnp.bfloat16)
    normed = (layer_norm(middle.astype(jnp.float32)) * is_valid[:, None]).astype(jnp.bfloat16)
    beside_all = time_rim(normed, conv_reach)
    conv_sum = jnp.zeros((frames, model_width), jnp.float32)
    for kernel_tap in range(conv_weight.shape[0]):
        conv_sum = conv_sum + conv_weight[kernel_tap] * beside_all[
            kernel_tap : kernel_tap + frames
        ].astype(jnp.float32)
    conv_out = (middle.astype(jnp.float32) + jax.nn.silu(conv_sum)).astype(jnp.bfloat16)
    ffn_in = layer_norm(conv_out.astype(jnp.float32)).astype(jnp.bfloat16)
    language = frame_lang[0]
    onehot = (
        (language[:, None] == jnp.arange(experts, dtype=jnp.int32)[None, :]) & is_valid[:, None]
    ).astype(jnp.int32)
    earlier = jnp.cumsum(onehot, axis=0) - onehot
    slot_index = jnp.sum(earlier * onehot, axis=1)
    is_kept = is_valid & (slot_index < slot_count)
    group = lax.axis_index("grp")
    count = experts // 2
    relative = (language - group) % count * 2 + (language // count ^ group // count)
    target = relative * slot_count + slot_index
    route_table = (
        (target[None, :] == jnp.arange(experts * slot_count, dtype=jnp.int32)[:, None])
        & is_kept[None, :]
    ).astype(jnp.bfloat16)
    outgoing = jnp.dot(route_table, ffn_in, preferred_element_type=jnp.float32).astype(jnp.bfloat16)
    hop = lambda v, ahead, is_other, is_return: group_hop(
        v, ahead, is_other, experts, places, stride, is_return
    )
    outgoing = outgoing.reshape(count, 2, slot_count, model_width)
    near = jnp.stack([outgoing[0]] + [hop(outgoing[i], i, 0, False) for i in range(1, count)])
    half = count * slot_count
    far_rows = hop(near[:, 1].reshape(half, model_width), 0, 1, False)
    own = jnp.concatenate([far_rows, near[:, 0].reshape(half, model_width)], axis=0)
    across = lambda i: (ring - 1 - i // stride) * stride + i % stride
    beside = lambda i: i ^ 1
    pair_rows = jnp.stack([own, place_hop(own, places, across)])
    all_rows = jnp.stack([pair_rows, place_hop(pair_rows, places, beside)])
    all_rows = all_rows.reshape(4, 2, half, model_width).swapaxes(0, 1).reshape(-1, model_width)
    partial = expert(all_rows, weights).reshape(2, 2, 2, half, model_width)

    def fold(part):
        mine = part[0] + place_hop(part[1].astype(jnp.bfloat16), places, beside).astype(jnp.float32)
        other = place_hop(mine[1].astype(jnp.bfloat16), places, across).astype(jnp.float32)
        return (mine[0] + other).astype(jnp.bfloat16)

    far_back = hop(fold(partial[0]), 0, 1, True).reshape(count, slot_count, model_width)
    near_back = fold(partial[1]).reshape(count, slot_count, model_width)
    back = jnp.stack([near_back, far_back], axis=1)
    returned = jnp.stack([back[0]] + [hop(back[i], i, 0, True) for i in range(1, count)])
    expert_out = lax.dot_general(
        route_table,
        returned.reshape(-1, model_width),
        (((0,), (0,)), ((), ())),
        preferred_element_type=jnp.float32,
    )
    output = is_valid[:, None] * (conv_out.astype(jnp.float32) + 0.5 * expert_out)
    return output.astype(jnp.bfloat16)[None]


def solution(mesh):
    in_specs = (
        P("grp", "tm", None),
        P("grp", "tm", None),
        P("grp", "tm", None),
        P("grp", "tm", None),
        P(),
        P("grp"),
        P("grp", "tm"),
        P("grp", None, "tm"),
        P("grp", "tm", None),
    )
    out_specs = P("grp", "tm", None)
    return jax.shard_map(body, mesh=mesh, in_specs=in_specs, out_specs=out_specs, check_vma=False)
```
